256 devices in a mesh: grp: 4 (over x_hi, core), pair: 64 (over y, x_lo, z).
Axes of the slice: x: 4 (x_hi: 2, x_lo: 2; x = x_hi * 2 + x_lo), y: 4, z: 8, core: 2. Of those that a mesh axis runs over, the one named last changes fastest.
Arguments:
- chol: bfloat16 [128, 1024, 1024], P(None, 'pair'), may hold values from -0.1875 to 0.1875
- trial: bfloat16 [1024, 512], replicated, may hold values from -2 to 2
- walkers: float32 [256, 1024, 512], P(('grp', 'pair')), may hold values from -10 to 10
- fields: float32 [256, 128], P('grp'), may hold values from -6 to 6
- weights: float32 [256], P(('grp', 'pair')), may hold values from 0.5 to 5
Outputs:
- new_walkers: float32 [256, 1024, 512], P(('grp', 'pair'))
- half_green: float32 [256, 1024, 512], P(('grp', 'pair'))
- new_weights: float32 [256], P(('grp', 'pair'))
The draws below stay inside these ranges and needn't reach their ends.
All inputs are finite; a program needn't handle non-finite values.
Results may differ from the reference program's by a relative error of at most 0.012.
The reference program's roundings to bfloat16 on the way (of `theta`, `green`, `shifted` and `operator`) count: a program that leaves them out, or rounds other values in their place, can miss the bound.
Values may be sent and summed in bfloat16 or wider, within the bound.
No kernel may reach another device: no remote copies, remote signals or barrier semaphores. Data moves between devices by JAX's collectives and lax.ppermute only.
A program may use at most 64 MiB of HBM per device.

```python
import jax
import jax.numpy as jnp
from jax import lax

M = 1024
N = 512
CHOL = 128
TAYLOR = 4
NS_ITERS = 3
WALKERS = 256


def draw_trial(key, part):
    first, second = jax.random.split(jax.random.fold_in(key, 11))
    top = jnp.eye(N, dtype=jnp.float32) + 0.15 * jnp.clip(jax.random.normal(first, (N, N), jnp.float32), -4.0, 4.0) / jnp.sqrt(float(N))
    bottom = 0.5 * jnp.clip(jax.random.normal(second, (M - N, N), jnp.float32), -4.0, 4.0) / jnp.sqrt(float(N))
    return jnp.concatenate([top, bottom], axis=0).astype(jnp.bfloat16)


def draw_walkers(key, part):
    first, second, third = jax.random.split(jax.random.fold_in(key, 23), 3)
    spread = 0.15
    scales = jnp.exp(jax.random.uniform(third, (WALKERS, 1, N), jnp.float32, 0.0, jnp.log(2.0)))
    top = jnp.eye(N, dtype=jnp.float32)[None] + spread * jnp.clip(jax.random.normal(first, (WALKERS, N, N), jnp.float32), -4.0, 4.0) / jnp.sqrt(float(N))
    bottom = 0.5 * jnp.clip(jax.random.normal(second, (WALKERS, M - N, N), jnp.float32), -4.0, 4.0) / jnp.sqrt(float(N))
    return jnp.concatenate([top, bottom], axis=1) * scales


def draw_weights(key, part):
    first = jax.random.fold_in(key, 37)
    steps = jnp.arange(WALKERS, dtype=jnp.float32) / max(WALKERS - 1, 1)
    base = jnp.exp(jnp.log(3.0) * steps)
    factor = jax.random.uniform(first, (WALKERS,), jnp.float32, 0.8, 1.25)
    return base * factor


def block_levels(rng, dims, shards, least, high):
    def one(position, blocks):
        steps = jax.random.uniform(jax.random.fold_in(jax.random.fold_in(rng, 6), position), (blocks,), jnp.float32, least / len(shards), high / len(shards))
        return jnp.repeat(jnp.exp(steps), dims[position] // blocks).reshape((-1,) + (1,) * (len(dims) - position - 1))

    loudness = one(*shards[0])
    for cut in shards[1:]:
        loudness = loudness * one(*cut)
    return loudness


def centred(rng, shape, width, most, cuts=(), kind=jnp.bfloat16):
    loudness = block_levels(rng, shape, cuts, -0.22, 0.18) if cuts else 1.0
    drawn = jax.random.normal(rng, shape, jnp.float32) * width * loudness
    return jnp.minimum(jnp.maximum(drawn, -most), most).astype(kind)


def setup_inputs(seed: int = 0) -> dict:
    keys = jax.random.split(jax.random.key(seed), 6)
    chol = centred(keys[0], (CHOL, M, M), (M * CHOL // 128) ** -0.5, 0.1875, ((1, 64),))
    trial = draw_trial(jax.random.fold_in(keys[5], 71), 0)
    walkers = draw_walkers(jax.random.fold_in(keys[5], 71), 0)
    fields = centred(keys[3], (WALKERS, CHOL), 1.0, 6.0, ((0, 4),), jnp.float32)
    weights = draw_weights(jax.random.fold_in(keys[5], 71), 0)
    return {"chol": chol, "trial": trial, "walkers": walkers, "fields": fields, "weights": weights}


root_step = 0.07


def newton(inner):
    entries = jnp.diagonal(inner)
    inverse = jnp.eye(N, dtype=jnp.float32) / entries[None, :]
    for sweep in range(NS_ITERS):
        product = jnp.dot(inner, inverse, precision=lax.Precision.HIGHEST)
        inverse = 2.0 * inverse - jnp.dot(inverse, product, precision=lax.Precision.HIGHEST)
    return inverse


def reference(chol, trial, walkers, fields, weights):
    trial_wide = trial.astype(jnp.float32)
    chol_flat = chol.reshape(CHOL, M * M)

    def one_walker(items):
        orbitals, draws, weight = items
        inner = jnp.dot(trial_wide.T, orbitals, precision=lax.Precision.HIGHEST)
        inverse = newton(inner)
        theta = jnp.dot(orbitals, inverse, precision=lax.Precision.HIGHEST).astype(jnp.bfloat16)
        green = jnp.dot(theta, trial.T, preferred_element_type=jnp.float32).astype(jnp.bfloat16)
        bias = jnp.dot(chol_flat, green.reshape(M * M), preferred_element_type=jnp.float32)
        xbar = -root_step * bias
        shifted = (draws - xbar).astype(jnp.bfloat16)
        operator = (root_step * jnp.dot(shifted, chol_flat, preferred_element_type=jnp.float32)).reshape(M, M).astype(jnp.bfloat16)
        term = orbitals
        total = orbitals
        for order in range(1, TAYLOR + 1):
            term = jnp.dot(operator, term.astype(jnp.bfloat16), preferred_element_type=jnp.float32) / float(order)
            total = total + term
        inner_next = jnp.dot(trial_wide.T, total, precision=lax.Precision.HIGHEST)
        inverse_next = newton(inner_next)
        half = jnp.dot(total, inverse_next, precision=lax.Precision.HIGHEST)
        raw = weight * jnp.exp(jnp.sum(draws * xbar - 0.5 * xbar * xbar))
        return total, half, raw

    new_walkers, half_green, raw = lax.map(one_walker, (walkers, fields, weights))
    new_weights = raw * (WALKERS / jnp.sum(raw))
    return new_walkers, half_green, new_weights
```

```python
import functools
import jax
import jax.numpy as jnp
from jax import lax
from jax.experimental import pallas as pl
from jax.experimental.pallas import tpu as pltpu
from jax.sharding import Mesh
from jax.sharding import PartitionSpec as P

TAYLOR = 4
root_step = 0.07
F32, BF16 = jnp.float32, jnp.bfloat16
NN = (((1,), (0,)), ((), ()))
NT = (((1,), (1,)), ((), ()))
TN = (((0,), (0,)), ((), ()))
VM = pltpu.VMEM
STEPS = 4


def mul(a, b, dims=NN):
    return lax.dot_general(a, b, dims, preferred_element_type=F32)


def pieces(x):
    high = x.astype(BF16)
    return high, (x - high.astype(F32)).astype(BF16)


def wide(a, b):
    (ah, al), (bh, bl) = a, b
    return mul(ah, bh) + (mul(ah, bl) + mul(al, bh))


def correction(inner, passes):
    size = inner.shape[0]
    row = lax.broadcasted_iota(jnp.int32, (size, size), 0)
    col = lax.broadcasted_iota(jnp.int32, (size, size), 1)
    on = row == col
    inv = 1.0 / jnp.sum(jnp.where(on, inner, 0.0), axis=0, keepdims=True)
    e1 = jnp.where(on, 1.0, 0.0) - inner * inv
    if passes == 3:
        p1 = pieces(e1)
        e2 = wide(p1, p1)
        p2 = pieces(e2)
        e3 = wide(p1, p2)
        e4 = wide(p2, p2)
        g = e1 + e2 + e3
        return inv, g + e4 + wide(pieces(g), pieces(e4))
    b1 = e1.astype(BF16)
    e2 = mul(b1, b1)
    b2 = e2.astype(BF16)
    e3 = mul(b1, b2)
    e4 = mul(b2, b2)
    g = e1 + e2 + e3
    return inv, g + e4 + mul(g.astype(BF16), e4.astype(BF16))


def apply_inverse(orbitals, inv, f, passes):
    scaled = orbitals * inv
    if passes == 3:
        return scaled + wide(pieces(scaled), pieces(f))
    return scaled + mul(scaled.astype(BF16), f.astype(BF16))


def inner_of(trial, orbitals):
    high, low = pieces(orbitals)
    return mul(trial, high, TN) + mul(trial, low, TN)


def theta_kernel(newton, last, trial, walkers, theta):
    w = walkers[...]
    inv, f = correction(inner_of(trial[...], w), newton)
    theta[...] = apply_inverse(w, inv, f, last).astype(BF16)


def theta_call(trial, walkers, newton=3, last=3):
    m, n = walkers.shape
    return pl.pallas_call(
        functools.partial(theta_kernel, newton, last),
        out_shape=jax.ShapeDtypeStruct((m, n), BF16),
        in_specs=[pl.BlockSpec(memory_space=VM)] * 2,
        out_specs=pl.BlockSpec(memory_space=VM),
        name="theta",
    )(trial, walkers)


def bias_kernel(theta, trial, chol, extra, out, rows, ordered, total):
    walkers, depth, n = theta.shape
    step = pl.program_id(0)

    @pl.when(step == 0)
    def _():
        for c in range(n // 128):
            lanes = pl.ds(c * 128, 128)
            rows[c] = theta[:, :, lanes].astype(F32).reshape(walkers * depth, 128)
        for r in range(depth):
            for c in range(n // 128):
                ordered[r * walkers : (r + 1) * walkers, c * 128 : (c + 1) * 128] = rows[
                    c, pl.ds(r, walkers, stride=depth), :
                ].astype(BF16)
        total[...] = jnp.zeros_like(total)

    green = mul(ordered[...], trial[...], NT).astype(BF16)
    part = total[...]
    for r in range(depth):
        part = part + mul(green[r * walkers : (r + 1) * walkers], chol[r], NT)
    total[...] = part

    @pl.when(step == pl.num_programs(0) - 1)
    def _():
        for c in range(out.shape[0]):
            out[c, :walkers, :] = part
            out[c, walkers:, :] = extra[...]


def bias_call(theta, trial, chol, extra, copies):
    walkers, depth, n = theta.shape
    _, vectors, width = chol.shape
    block = width // STEPS
    return pl.pallas_call(
        bias_kernel,
        grid=(STEPS,),
        out_shape=jax.ShapeDtypeStruct((copies, walkers + 8, vectors), F32),
        in_specs=[
            pl.BlockSpec((walkers, depth, n), lambda q: (0, 0, 0)),
            pl.BlockSpec((block, n), lambda q: (q, 0)),
            pl.BlockSpec((depth, vectors, block), lambda q: (0, 0, q)),
            pl.BlockSpec((8, vectors), lambda q: (0, 0)),
        ],
        out_specs=pl.BlockSpec((copies, walkers + 8, vectors), lambda q: (0, 0, 0)),
        scratch_shapes=[
            VM((n // 128, walkers * depth, 128), F32),
            VM((walkers * depth, n), BF16),
            VM((walkers, vectors), F32),
        ],
        name="bias",
    )(theta, trial, chol, extra)


def spread_kernel(parts, out):
    total = jnp.sum(parts[...], axis=0)
    for c in range(out.shape[0]):
        out[c] = total


def spread_call(parts, copies):
    return pl.pallas_call(
        spread_kernel,
        out_shape=jax.ShapeDtypeStruct((copies,) + parts.shape[1:], F32),
        in_specs=[pl.BlockSpec(memory_space=VM)],
        out_specs=pl.BlockSpec(memory_space=VM),
        name="spread",
    )(parts)


def operator_kernel(parts, fields, chol, operator, summed, rows, shifted):
    walkers = fields.shape[0]
    depth = chol.shape[0]

    @pl.when(pl.program_id(0) == 0)
    def _():
        total = jnp.sum(parts[...], axis=0)
        summed[...] = total
        shifted[...] = (fields[...] + root_step * total[:walkers]).astype(BF16)

    for r in range(depth):
        block = root_step * mul(shifted[...], chol[r])
        for c in range(rows.shape[0]):
            rows[c, pl.ds(r, walkers, stride=depth), :] = block[:, c * 128 : (c + 1) * 128]
    for c in range(rows.shape[0]):
        lanes = pl.ds(c * 128, 128)
        operator[:, :, lanes] = rows[c].astype(BF16).reshape(walkers, depth, 128)


def operator_call(parts, fields, chol):
    walkers = fields.shape[0]
    depth, vectors, width = chol.shape
    block = width // STEPS
    return pl.pallas_call(
        operator_kernel,
        grid=(STEPS,),
        out_shape=(
            jax.ShapeDtypeStruct((walkers, depth, width), BF16),
            jax.ShapeDtypeStruct(parts.shape[1:], F32),
        ),
        in_specs=[
            pl.BlockSpec(parts.shape, lambda q: (0, 0, 0)),
            pl.BlockSpec(fields.shape, lambda q: (0, 0)),
            pl.BlockSpec((depth, vectors, block), lambda q: (0, 0, q)),
        ],
        out_specs=(
            pl.BlockSpec((walkers, depth, block), lambda q: (0, 0, q)),
            pl.BlockSpec(parts.shape[1:], lambda q: (0, 0)),
        ),
        scratch_shapes=[
            VM((block // 128, walkers * depth, 128), F32),
            VM(fields.shape, BF16),
        ],
        name="operator",
    )(parts, fields, chol)


def step_kernel(newton, last, operator, trial, walkers, total, half, now, sem):
    term = walkers[...].astype(BF16)
    full = walkers[...]
    for order in range(1, TAYLOR + 1):
        fresh = mul(operator[...], term) / float(order)
        full = full + fresh
        term = fresh.astype(BF16)
    now[...] = full
    copy = pltpu.make_async_copy(now, total, sem)
    copy.start()
    inv, f = correction(inner_of(trial[...], now[...]), newton)
    half[...] = apply_inverse(now[...], inv, f, last)
    copy.wait()


def step_call(operator, trial, walkers, newton=3, last=3):
    return pl.pallas_call(
        functools.partial(step_kernel, newton, last),
        out_shape=(jax.ShapeDtypeStruct(walkers.shape, F32),) * 2,
        in_specs=[pl.BlockSpec(memory_space=VM)] * 3,
        out_specs=(pl.BlockSpec(memory_space=pl.ANY), pl.BlockSpec(memory_space=VM)),
        scratch_shapes=[VM(walkers.shape, F32), pltpu.SemaphoreType.DMA],
        name="step",
    )(operator, trial, walkers)


PAIR = ("pair_0", "pair_1", "pair_2")
GRP = ("grp_0", "grp_1")
NEAR = ("pair_0", "pair_1")
FAR = ("pair_2",)


def swap(array, axes):
    return lax.all_to_all(array, axes, split_axis=0, concat_axis=0, tiled=True)


def per_device(chol, trial, walkers, fields, weights):
    _, m, n = walkers.shape
    vectors, depth, _ = chol.shape
    group = lax.axis_size(PAIR)
    place = lax.axis_index(PAIR)
    orbitals = walkers[0]
    theta = theta_call(trial, orbitals).reshape(group, depth, n)
    theta_block = swap(theta, PAIR)
    by_row = jnp.transpose(chol, (1, 0, 2))
    row = lax.broadcasted_iota(jnp.int32, (8, vectors), 0)
    lane = lax.broadcasted_iota(jnp.int32, (8, vectors), 1)
    extra = jnp.where((row == 0) & (lane == place), weights[0], 0.0)
    parts = bias_call(theta_block, trial, by_row, extra, lax.axis_size(FAR))
    parts = spread_call(swap(parts, FAR), lax.axis_size(NEAR))
    op_block, summed = operator_call(swap(parts, NEAR), fields, by_row)
    operator = swap(op_block, PAIR).reshape(m, m)
    total, half_green = step_call(operator, trial, orbitals)
    xbar = -root_step * summed[:group]
    growth = jnp.exp(jnp.sum(fields * xbar - 0.5 * xbar * xbar, axis=1))
    whole = jnp.sum(summed[group, :group] * growth)
    for axis in GRP:
        whole = lax.psum(whole, axis)
    raw = weights * lax.dynamic_slice_in_dim(growth, place, 1, 0)
    new_weights = raw * (group * lax.axis_size(GRP) / whole)
    return (total[None], half_green[None], new_weights)


def solution(mesh):
    torus = Mesh(
        mesh.devices.reshape(2, 2, 4, 2, 8), ("grp_0", "grp_1", "pair_0", "pair_1", "pair_2")
    )
    every = GRP + PAIR
    return jax.shard_map(
        per_device,
        mesh=torus,
        in_specs=(P(None, PAIR, None), P(), P(every, None, None), P(GRP, None), P(every)),
        out_specs=(P(every, None, None), P(every, None, None), P(every)),
        check_vma=False,
    )
```

```python
import functools

import jax
import jax.numpy as jnp
from jax import lax
from jax.experimental import pallas as pl
from jax.experimental.pallas import tpu as pltpu
from jax.sharding import Mesh
from jax.sharding import PartitionSpec as P

TAYLOR = 4
PAIR = ("pair_0", "pair_1", "pair_2")
GRP = ("grp_0", "grp_1")
NEAR = ("pair_0", "pair_1")
FAR = ("pair_2",)
TURN = 2000
PIECES = 4

root_step = 0.07

F32, BF16 = jnp.float32, jnp.bfloat16
NN = (((1,), (0,)), ((), ()))
NT = (((1,), (1,)), ((), ()))
TN = (((0,), (0,)), ((), ()))
VM = pltpu.VMEM
HERE = pl.BlockSpec(memory_space=pltpu.VMEM)
AWAY = pl.BlockSpec(memory_space=pltpu.HBM)


def near(*arrays):
    return [pltpu.with_memory_space_constraint(a, pltpu.VMEM) for a in arrays]


def away(*arrays):
    return [pltpu.with_memory_space_constraint(a, pltpu.HBM) for a in arrays]


def grant(mib):
    return pltpu.CompilerParams(vmem_limit_bytes=mib << 20)


def mul(a, b, dims=NN):
    return lax.dot_general(a, b, dims, preferred_element_type=F32)


def short(a, b):
    return mul(a.astype(BF16), b.astype(BF16))


def inner_of(trial, orbitals):
    high = orbitals.astype(BF16)
    low = (orbitals - high.astype(F32)).astype(BF16)
    return mul(trial, high, TN) + mul(trial, low, TN)


def correction(inner):
    size = inner.shape[0]
    row = lax.broadcasted_iota(jnp.int32, (size, size), 0)
    col = lax.broadcasted_iota(jnp.int32, (size, size), 1)
    on = row == col
    inv = 1.0 / jnp.sum(jnp.where(on, inner, 0.0), axis=0, keepdims=True)
    e1 = jnp.where(on, 1.0, 0.0) - inner * inv
    e2 = short(e1, e1)
    e4 = short(e2, e2)
    g = e1 + e2 + short(e1, e2)
    return inv, g + e4 + short(g, e4)


def theta_kernel(turn, trial_hbm, walkers_hbm, theta, trial, walkers, idle, sems):
    rows = walkers.shape[0] // PIECES
    parts = [pl.ds(c * rows, rows) for c in range(PIECES)]
    copies = []
    for c, part in enumerate(parts):
        copies.append(
            (
                pltpu.make_async_copy(trial_hbm.at[part], trial.at[part], sems.at[0, c]),
                pltpu.make_async_copy(walkers_hbm.at[part], walkers.at[part], sems.at[1, c]),
            )
        )
        for copy in copies[-1]:
            copy.start()
    inner = None
    for c, part in enumerate(parts):
        for copy in copies[c]:
            copy.wait()
        piece = inner_of(trial[part, :], walkers[part, :])
        inner = piece if inner is None else inner + piece
    inv, f = correction(inner)
    scaled = walkers[...] * inv
    theta[...] = (scaled + short(scaled, f)).astype(BF16)
    if TURN:
        idle[...] = jnp.zeros_like(idle)

        def wait(_, carry):
            idle[...] = idle[...] + 1.0
            return carry

        lax.fori_loop(0, turn[0] * TURN, wait, 0)


def theta_call(turn, trial, walkers):
    m, n = walkers.shape
    return pl.pallas_call(
        theta_kernel,
        out_shape=jax.ShapeDtypeStruct((m, n), BF16),
        in_specs=[pl.BlockSpec(memory_space=pltpu.SMEM), AWAY, AWAY],
        out_specs=HERE,
        scratch_shapes=[
            VM(trial.shape, BF16),
            VM(walkers.shape, F32),
            VM((8, 128), F32),
            pltpu.SemaphoreType.DMA((2, PIECES)),
        ],
        compiler_params=grant(24),
        name="theta",
    )(turn, *away(trial, walkers))


def ready_kernel(chol_hbm, trial, flat_hbm, met_hbm, chol, flat, met, loads, stores):
    vectors, depth, width = chol.shape
    n = trial.shape[1]
    some = vectors // PIECES
    copies = []
    for c in range(PIECES):
        part = pl.ds(c * some, some)
        copies.append(pltpu.make_async_copy(chol_hbm.at[part], chol.at[part], loads.at[c]))
        copies[-1].start()
    sent = []
    for c in range(PIECES):
        part = pl.ds(c * some, some)
        copies[c].wait()
        turned = jnp.swapaxes(chol[part], 0, 1)
        for r in range(depth):
            flat[part, r * width : (r + 1) * width] = turned[r]
        sent.append(pltpu.make_async_copy(flat.at[part], flat_hbm.at[part], stores.at[0, c]))
        sent[-1].start()
        product = mul(turned.reshape(depth * some, width), trial[...]).astype(BF16)
        for r in range(depth):
            met[part, r * n : (r + 1) * n] = product[r * some : (r + 1) * some]
        sent.append(pltpu.make_async_copy(met.at[part], met_hbm.at[part], stores.at[1, c]))
        sent[-1].start()
    for copy in sent:
        copy.wait()


def ready_call(chol, trial):
    vectors, depth, width = chol.shape
    n = trial.shape[1]
    return pl.pallas_call(
        ready_kernel,
        out_shape=(
            pltpu.HBM((vectors, depth * width), BF16),
            pltpu.HBM((vectors, depth * n), BF16),
        ),
        in_specs=[AWAY, HERE],
        out_specs=(AWAY, AWAY),
        scratch_shapes=[
            VM(chol.shape, BF16),
            VM((vectors, depth * width), BF16),
            VM((vectors, depth * n), BF16),
            pltpu.SemaphoreType.DMA((PIECES,)),
            pltpu.SemaphoreType.DMA((2, PIECES)),
        ],
        compiler_params=grant(24),
        name="ready",
    )(*away(chol), *near(trial))


def bias_kernel(theta, met_hbm, extra, out, rows, met, sems):
    walkers, depth, n = theta.shape
    some = met.shape[0] // PIECES
    copies = []
    for c in range(PIECES):
        part = pl.ds(c * some, some)
        copies.append(pltpu.make_async_copy(met_hbm.at[part], met.at[part], sems.at[c]))
        copies[-1].start()
    turned = jnp.swapaxes(theta[...], 0, 1)
    for r in range(depth):
        rows[:, r * n : (r + 1) * n] = turned[r]
    for copy in copies:
        copy.wait()
    total = mul(rows[...], met[...], NT).astype(out.dtype)
    for c in range(out.shape[0]):
        out[c, :walkers, :] = total
        out[c, walkers:, :] = extra[...]


def bias_call(theta, met, extra, copies):
    walkers, depth, n = theta.shape
    vectors = met.shape[0]
    return pl.pallas_call(
        bias_kernel,
        out_shape=jax.ShapeDtypeStruct((copies, walkers + extra.shape[0], vectors), extra.dtype),
        in_specs=[HERE, AWAY, HERE],
        out_specs=HERE,
        scratch_shapes=[
            VM((walkers, depth * n), BF16),
            VM(met.shape, BF16),
            pltpu.SemaphoreType.DMA((PIECES,)),
        ],
        compiler_params=grant(16),
        name="bias",
    )(*near(theta), *away(met), *near(extra))


def spread_kernel(parts, out):
    total = jnp.sum(parts[...].astype(F32), axis=0).astype(out.dtype)
    for c in range(out.shape[0]):
        out[c] = total


def spread_call(parts, copies):
    return pl.pallas_call(
        spread_kernel,
        out_shape=jax.ShapeDtypeStruct((copies,) + parts.shape[1:], parts.dtype),
        in_specs=[HERE],
        out_specs=HERE,
        compiler_params=grant(8),
        name="spread",
    )(*near(parts))


def operator_kernel(parts, fields, chol, operator, summed, rows, turned, sems):
    total = jnp.sum(parts[...].astype(F32), axis=0)
    summed[...] = total
    walkers, depth, width = operator.shape
    shifted = (fields[...] + root_step * total[:walkers]).astype(BF16)
    flat = (root_step * mul(shifted, chol[...])).astype(BF16)
    for r in range(depth):
        rows[r] = flat[:, r * width : (r + 1) * width]
    some = walkers // PIECES
    copies = []
    for c in range(PIECES):
        part = pl.ds(c * some, some)
        turned[part] = jnp.swapaxes(rows[:, part, :], 0, 1)
        copies.append(pltpu.make_async_copy(turned.at[part], operator.at[part], sems.at[c]))
        copies[-1].start()
    for copy in copies:
        copy.wait()


def operator_call(parts, fields, chol, depth):
    walkers = fields.shape[0]
    width = chol.shape[1] // depth
    return pl.pallas_call(
        operator_kernel,
        out_shape=(
            pltpu.HBM((walkers, depth, width), BF16),
            jax.ShapeDtypeStruct(parts.shape[1:], F32),
        ),
        in_specs=[HERE] * 3,
        out_specs=(AWAY, HERE),
        scratch_shapes=[
            VM((depth, walkers, width), BF16),
            VM((walkers, depth, width), BF16),
            pltpu.SemaphoreType.DMA((PIECES,)),
        ],
        compiler_params=grant(20),
        name="operator",
    )(*near(parts, fields, chol))


def step_kernel(operator_hbm, trial, walkers, total, half, operator, term, now, done, sems):
    size, n = walkers.shape
    blocks, depth, _ = operator.shape
    some = blocks // PIECES
    rows = size // PIECES
    parts = [pl.ds(c * rows, rows) for c in range(PIECES)]
    copies = []
    for c in range(PIECES):
        part = pl.ds(c * some, some)
        copies.append(
            pltpu.make_async_copy(operator_hbm.at[part], operator.at[part], sems.at[0, c])
        )
        copies[-1].start()
    start = walkers[...].astype(BF16)
    for c, part in enumerate(parts):
        copies[c].wait()
        fresh = mul(operator[c * some : (c + 1) * some].reshape(rows, size), start)
        term[part, :] = fresh.astype(BF16)
        now[part, :] = walkers[part, :] + fresh
    full = now[...]
    last = term[...]
    for order in range(2, TAYLOR + 1):
        fresh = mul(operator[...].reshape(size, size), last) / float(order)
        full = full + fresh
        last = fresh.astype(BF16)
    now[...] = full
    copies = [pltpu.make_async_copy(now, total, sems.at[1, PIECES])]
    copies[0].start()
    inv, f = correction(inner_of(trial[...], now[...]))
    for c, part in enumerate(parts):
        scaled = now[part, :] * inv
        done[part, :] = scaled + short(scaled, f)
        copies.append(pltpu.make_async_copy(done.at[part, :], half.at[part, :], sems.at[1, c]))
        copies[-1].start()
    for copy in copies:
        copy.wait()


def step_call(operator, trial, walkers):
    return pl.pallas_call(
        step_kernel,
        out_shape=(jax.ShapeDtypeStruct(walkers.shape, F32),) * 2,
        in_specs=[AWAY, HERE, HERE],
        out_specs=(AWAY, AWAY),
        scratch_shapes=[
            VM(operator.shape, BF16),
            VM(walkers.shape, BF16),
            VM(walkers.shape, F32),
            VM(walkers.shape, F32),
            pltpu.SemaphoreType.DMA((2, PIECES + 1)),
        ],
        compiler_params=grant(30),
        name="step",
    )(*away(operator), *near(trial, walkers))


def swap(array, axes):
    return lax.all_to_all(array, axes, split_axis=0, concat_axis=0, tiled=True)


def per_device(chol, trial, walkers, fields, weights):
    _, _, n = walkers.shape
    vectors, depth, _ = chol.shape
    group = lax.axis_size(PAIR)
    place = lax.axis_index(PAIR)
    orbitals = walkers[0]
    turn = lax.axis_index("grp_1").astype(jnp.int32).reshape(1)
    theta = theta_call(turn, trial, orbitals).reshape(group, depth, n)
    theta_block = swap(theta, PAIR)
    flat, met = ready_call(chol, trial)
    row = lax.broadcasted_iota(jnp.int32, (16, vectors), 0)
    lane = lax.broadcasted_iota(jnp.int32, (16, vectors), 1)
    weight = weights[0]
    high = lax.reduce_precision(weight, 8, 7)
    middle = lax.reduce_precision(weight - high, 8, 7)
    low = weight - high - middle
    pieces = jnp.where(row == 0, high, jnp.where(row == 1, middle, jnp.where(row == 2, low, 0.0)))
    extra = jnp.where(lane == place, pieces, 0.0).astype(BF16)
    parts = bias_call(theta_block, met, extra, lax.axis_size(FAR))
    parts, later = lax.optimization_barrier((parts, flat))
    parts = spread_call(swap(parts, FAR), lax.axis_size(NEAR))
    op_block, summed = operator_call(swap(parts, NEAR), fields, later, depth)
    operator = swap(op_block, PAIR)
    total, half_green = step_call(operator, trial, orbitals)
    xbar = -root_step * summed[:group]
    growth = jnp.exp(jnp.sum(fields * xbar - 0.5 * xbar * xbar, axis=1))
    whole = jnp.sum(jnp.sum(summed[group:, :group], axis=0) * growth)
    for axis in GRP:
        whole = lax.psum(whole, axis)
    raw = weights * lax.dynamic_slice_in_dim(growth, place, 1, 0)
    new_weights = raw * (group * lax.axis_size(GRP) / whole)
    return (total[None], half_green[None], new_weights)


def solution(mesh):
    torus = Mesh(
        mesh.devices.reshape(2, 2, 4, 2, 8), ("grp_0", "grp_1", "pair_0", "pair_1", "pair_2")
    )
    every = GRP + PAIR
    return jax.shard_map(
        per_device,
        mesh=torus,
        in_specs=(P(None, PAIR, None), P(), P(every, None, None), P(GRP, None), P(every)),
        out_specs=(P(every, None, None), P(every, None, None), P(every)),
        check_vma=False,
    )
```

```python
import functools

import jax
import jax.numpy as jnp
from jax import lax
from jax.experimental import pallas as pl
from jax.experimental.pallas import tpu as pltpu
from jax.sharding import Mesh
from jax.sharding import PartitionSpec as P

TAYLOR = 4
PAIR = ("pair_0", "pair_1", "pair_2")
GRP = ("grp_0", "grp_1")
NEAR = ("pair_0", "pair_1")
FAR = ("pair_2",)
TURN = 2000
PIECES = 4
LOADS = 2

root_step = 0.07

F32, BF16 = jnp.float32, jnp.bfloat16
NN = (((1,), (0,)), ((), ()))
NT = (((1,), (1,)), ((), ()))
TN = (((0,), (0,)), ((), ()))
VM = pltpu.VMEM
HERE = pl.BlockSpec(memory_space=pltpu.VMEM)
AWAY = pl.BlockSpec(memory_space=pltpu.HBM)


def near(*arrays):
    return [pltpu.with_memory_space_constraint(a, pltpu.VMEM) for a in arrays]


def away(*arrays):
    return [pltpu.with_memory_space_constraint(a, pltpu.HBM) for a in arrays]


def grant(mib):
    return pltpu.CompilerParams(vmem_limit_bytes=mib << 20)


def mul(a, b, dims=NN):
    return lax.dot_general(a, b, dims, preferred_element_type=F32)


def short(a, b):
    return mul(a.astype(BF16), b.astype(BF16))


def inner_of(trial, orbitals):
    high = orbitals.astype(BF16)
    low = (orbitals - high.astype(F32)).astype(BF16)
    return mul(trial, high, TN) + mul(trial, low, TN)


def correction(inner):
    size = inner.shape[0]
    row = lax.broadcasted_iota(jnp.int32, (size, size), 0)
    col = lax.broadcasted_iota(jnp.int32, (size, size), 1)
    on = row == col
    inv = 1.0 / jnp.sum(jnp.where(on, inner, 0.0), axis=0, keepdims=True)
    e1 = jnp.where(on, 1.0, 0.0) - inner * inv
    b1 = e1.astype(BF16)
    e2 = mul(b1, b1)
    b2 = e2.astype(BF16)
    both = mul(jnp.concatenate([b1, b2], axis=0), b2)
    g = e1 + e2 + both[:size]
    e4 = both[size:]
    return inv, g + e4 + short(g, e4)


def theta_kernel(turn, trial_hbm, walkers_hbm, theta, trial, walkers, idle, sems):
    rows = walkers.shape[0] // PIECES
    parts = [pl.ds(c * rows, rows) for c in range(PIECES)]
    copies = []
    for c, part in enumerate(parts):
        copies.append(
            (
                pltpu.make_async_copy(trial_hbm.at[part], trial.at[part], sems.at[0, c]),
                pltpu.make_async_copy(walkers_hbm.at[part], walkers.at[part], sems.at[1, c]),
            )
        )
        for copy in copies[-1]:
            copy.start()
    inner = None
    for c, part in enumerate(parts):
        for copy in copies[c]:
            copy.wait()
        piece = inner_of(trial[part, :], walkers[part, :])
        inner = piece if inner is None else inner + piece
    inv, f = correction(inner)
    scaled = walkers[...] * inv
    theta[...] = (scaled + short(scaled, f)).astype(BF16)
    if TURN:
        idle[...] = jnp.zeros_like(idle)

        def wait(_, carry):
            idle[...] = idle[...] + 1.0
            return carry

        lax.fori_loop(0, turn[0] * TURN, wait, 0)


def theta_call(turn, trial, walkers):
    m, n = walkers.shape
    return pl.pallas_call(
        theta_kernel,
        out_shape=jax.ShapeDtypeStruct((m, n), BF16),
        in_specs=[pl.BlockSpec(memory_space=pltpu.SMEM), AWAY, AWAY],
        out_specs=HERE,
        scratch_shapes=[
            VM(trial.shape, BF16),
            VM(walkers.shape, F32),
            VM((8, 128), F32),
            pltpu.SemaphoreType.DMA((2, PIECES)),
        ],
        compiler_params=grant(24),
        name="theta",
    )(turn, *away(trial, walkers))


def ready_kernel(chol_hbm, trial, flat_hbm, met_hbm, chol, flat, met, loads, stores):
    vectors, depth, width = chol.shape
    n = trial.shape[1]
    some = vectors // PIECES
    copies = []
    for c in range(PIECES):
        part = pl.ds(c * some, some)
        copies.append(pltpu.make_async_copy(chol_hbm.at[part], chol.at[part], loads.at[c]))
        copies[-1].start()
    sent = []
    for c in range(PIECES):
        part = pl.ds(c * some, some)
        copies[c].wait()
        turned = jnp.swapaxes(chol[part], 0, 1)
        for r in range(depth):
            flat[part, r * width : (r + 1) * width] = turned[r]
        sent.append(pltpu.make_async_copy(flat.at[part], flat_hbm.at[part], stores.at[0, c]))
        sent[-1].start()
        product = mul(turned.reshape(depth * some, width), trial[...]).astype(BF16)
        for r in range(depth):
            met[part, r * n : (r + 1) * n] = product[r * some : (r + 1) * some]
        sent.append(pltpu.make_async_copy(met.at[part], met_hbm.at[part], stores.at[1, c]))
        sent[-1].start()
    for copy in sent:
        copy.wait()


def ready_call(chol, trial):
    vectors, depth, width = chol.shape
    n = trial.shape[1]
    return pl.pallas_call(
        ready_kernel,
        out_shape=(
            pltpu.HBM((vectors, depth * width), BF16),
            pltpu.HBM((vectors, depth * n), BF16),
        ),
        in_specs=[AWAY, HERE],
        out_specs=(AWAY, AWAY),
        scratch_shapes=[
            VM(chol.shape, BF16),
            VM((vectors, depth * width), BF16),
            VM((vectors, depth * n), BF16),
            pltpu.SemaphoreType.DMA((PIECES,)),
            pltpu.SemaphoreType.DMA((2, PIECES)),
        ],
        compiler_params=grant(24),
        name="ready",
    )(*away(chol), *near(trial))


def bias_kernel(theta, met_hbm, extra, out, rows, met, sems):
    walkers, depth, n = theta.shape
    some = met.shape[0] // PIECES
    copies = []
    for c in range(PIECES):
        part = pl.ds(c * some, some)
        copies.append(pltpu.make_async_copy(met_hbm.at[part], met.at[part], sems.at[c]))
        copies[-1].start()
    turned = jnp.swapaxes(theta[...], 0, 1)
    for r in range(depth):
        rows[:, r * n : (r + 1) * n] = turned[r]
    for copy in copies:
        copy.wait()
    total = mul(rows[...], met[...], NT).astype(out.dtype)
    for c in range(out.shape[0]):
        out[c, :walkers, :] = total
        out[c, walkers:, :] = extra[...]


def bias_call(theta, met, extra, copies):
    walkers, depth, n = theta.shape
    vectors = met.shape[0]
    return pl.pallas_call(
        bias_kernel,
        out_shape=jax.ShapeDtypeStruct((copies, walkers + extra.shape[0], vectors), extra.dtype),
        in_specs=[HERE, AWAY, HERE],
        out_specs=HERE,
        scratch_shapes=[
            VM((walkers, depth * n), BF16),
            VM(met.shape, BF16),
            pltpu.SemaphoreType.DMA((PIECES,)),
        ],
        compiler_params=grant(16),
        name="bias",
    )(*near(theta), *away(met), *near(extra))


def spread_kernel(parts, out):
    total = jnp.sum(parts[...].astype(F32), axis=0).astype(out.dtype)
    for c in range(out.shape[0]):
        out[c] = total


def spread_call(parts, copies):
    return pl.pallas_call(
        spread_kernel,
        out_shape=jax.ShapeDtypeStruct((copies,) + parts.shape[1:], parts.dtype),
        in_specs=[HERE],
        out_specs=HERE,
        compiler_params=grant(8),
        name="spread",
    )(*near(parts))


def operator_kernel(parts, fields, chol, operator, summed, rows, turned, sems):
    total = jnp.sum(parts[...].astype(F32), axis=0)
    summed[...] = total
    walkers, depth, width = operator.shape
    shifted = (fields[...] + root_step * total[:walkers]).astype(BF16)
    some = width // PIECES
    copies = []
    for c in range(PIECES):
        part = pl.ds(c * some, some)
        for r in range(depth):
            start = r * width + c * some
            rows[r, :, part] = (root_step * mul(shifted, chol[:, start : start + some])).astype(BF16)
        turned[:, :, part] = jnp.swapaxes(rows[:, :, part], 0, 1)
        copies.append(pltpu.make_async_copy(turned.at[:, :, part], operator.at[:, :, part], sems.at[c]))
        copies[-1].start()
    for copy in copies:
        copy.wait()


def operator_call(parts, fields, chol, depth):
    walkers = fields.shape[0]
    width = chol.shape[1] // depth
    return pl.pallas_call(
        operator_kernel,
        out_shape=(
            pltpu.HBM((walkers, depth, width), BF16),
            jax.ShapeDtypeStruct(parts.shape[1:], F32),
        ),
        in_specs=[HERE] * 3,
        out_specs=(AWAY, HERE),
        scratch_shapes=[
            VM((depth, walkers, width), BF16),
            VM((walkers, depth, width), BF16),
            pltpu.SemaphoreType.DMA((PIECES,)),
        ],
        compiler_params=grant(20),
        name="operator",
    )(*near(parts, fields, chol))


def step_kernel(operator_hbm, trial, walkers, total, half, operator, term, now, done, sems):
    size, n = walkers.shape
    blocks, depth, _ = operator.shape
    rows = size // PIECES
    parts = [pl.ds(c * rows, rows) for c in range(PIECES)]
    some = blocks // LOADS
    tall = size // LOADS
    copies = []
    for c in range(LOADS):
        part = pl.ds(c * some, some)
        copies.append(
            pltpu.make_async_copy(operator_hbm.at[part], operator.at[part], sems.at[0, c])
        )
        copies[-1].start()
    start = walkers[...].astype(BF16)
    for c in range(LOADS):
        part = pl.ds(c * tall, tall)
        copies[c].wait()
        fresh = mul(operator[c * some : (c + 1) * some].reshape(tall, size), start)
        term[part, :] = fresh.astype(BF16)
        now[part, :] = walkers[part, :] + fresh
    full = now[...]
    last = term[...]
    for order in range(2, TAYLOR + 1):
        fresh = mul(operator[...].reshape(size, size), last) / float(order)
        full = full + fresh
        last = fresh.astype(BF16)
    now[...] = full
    copies = [pltpu.make_async_copy(now, total, sems.at[1, PIECES])]
    copies[0].start()
    inv, f = correction(inner_of(trial[...], now[...]))
    for c, part in enumerate(parts):
        scaled = now[part, :] * inv
        done[part, :] = scaled + short(scaled, f)
        copies.append(pltpu.make_async_copy(done.at[part, :], half.at[part, :], sems.at[1, c]))
        copies[-1].start()
    for copy in copies:
        copy.wait()


def step_call(operator, trial, walkers):
    return pl.pallas_call(
        step_kernel,
        out_shape=(jax.ShapeDtypeStruct(walkers.shape, F32),) * 2,
        in_specs=[AWAY, HERE, HERE],
        out_specs=(AWAY, AWAY),
        scratch_shapes=[
            VM(operator.shape, BF16),
            VM(walkers.shape, BF16),
            VM(walkers.shape, F32),
            VM(walkers.shape, F32),
            pltpu.SemaphoreType.DMA((2, PIECES + 1)),
        ],
        compiler_params=grant(30),
        name="step",
    )(*away(operator), *near(trial, walkers))


def swap(array, axes):
    return lax.all_to_all(array, axes, split_axis=0, concat_axis=0, tiled=True)


def per_device(chol, trial, walkers, fields, weights):
    _, _, n = walkers.shape
    vectors, depth, _ = chol.shape
    group = lax.axis_size(PAIR)
    place = lax.axis_index(PAIR)
    orbitals = walkers[0]
    turn = lax.axis_index("grp_1").astype(jnp.int32).reshape(1)
    theta = theta_call(turn, trial, orbitals).reshape(group, depth, n)
    theta_block = swap(theta, PAIR)
    flat, met = ready_call(chol, trial)
    row = lax.broadcasted_iota(jnp.int32, (16, vectors), 0)
    lane = lax.broadcasted_iota(jnp.int32, (16, vectors), 1)
    weight = weights[0]
    high = lax.reduce_precision(weight, 8, 7)
    middle = lax.reduce_precision(weight - high, 8, 7)
    low = weight - high - middle
    pieces = jnp.where(row == 0, high, jnp.where(row == 1, middle, jnp.where(row == 2, low, 0.0)))
    extra = jnp.where(lane == place, pieces, 0.0).astype(BF16)
    parts = bias_call(theta_block, met, extra, lax.axis_size(FAR))
    parts = spread_call(swap(parts, FAR), lax.axis_size(NEAR))
    op_block, summed = operator_call(swap(parts, NEAR), fields, flat, depth)
    operator = swap(op_block, PAIR)
    total, half_green = step_call(operator, trial, orbitals)
    xbar = -root_step * summed[:group]
    growth = jnp.exp(jnp.sum(fields * xbar - 0.5 * xbar * xbar, axis=1))
    whole = jnp.sum(jnp.sum(summed[group:, :group], axis=0) * growth)
    for axis in GRP:
        whole = lax.psum(whole, axis)
    raw = weights * lax.dynamic_slice_in_dim(growth, place, 1, 0)
    new_weights = raw * (group * lax.axis_size(GRP) / whole)
    return (total[None], half_green[None], new_weights)


def solution(mesh):
    torus = Mesh(
        mesh.devices.reshape(2, 2, 4, 2, 8), ("grp_0", "grp_1", "pair_0", "pair_1", "pair_2")
    )
    every = GRP + PAIR
    return jax.shard_map(
        per_device,
        mesh=torus,
        in_specs=(P(None, PAIR, None), P(), P(every, None, None), P(GRP, None), P(every)),
        out_specs=(P(every, None, None), P(every, None, None), P(every)),
        check_vma=False,
    )
```

```python
import functools

import jax
import jax.numpy as jnp
from jax import lax
from jax.experimental import pallas as pl
from jax.experimental.pallas import tpu as pltpu
from jax.sharding import Mesh
from jax.sharding import PartitionSpec as P

TAYLOR = 4
PAIR = ("pair_0", "pair_1", "pair_2")
GRP = ("grp_0", "grp_1")
NEAR = ("pair_0", "pair_1")
FAR = ("pair_2",)
TURN = 2000
PIECES = 4
LOADS = 2

root_step = 0.07

F32, BF16 = jnp.float32, jnp.bfloat16
NN = (((1,), (0,)), ((), ()))
NT = (((1,), (1,)), ((), ()))
TN = (((0,), (0,)), ((), ()))
VM = pltpu.VMEM
HERE = pl.BlockSpec(memory_space=pltpu.VMEM)
AWAY = pl.BlockSpec(memory_space=pltpu.HBM)


def near(*arrays):
    return [pltpu.with_memory_space_constraint(a, pltpu.VMEM) for a in arrays]


def away(*arrays):
    return [pltpu.with_memory_space_constraint(a, pltpu.HBM) for a in arrays]


def grant(mib):
    return pltpu.CompilerParams(vmem_limit_bytes=mib << 20)


def mul(a, b, dims=NN):
    return lax.dot_general(a, b, dims, preferred_element_type=F32)


def short(a, b):
    return mul(a.astype(BF16), b.astype(BF16))


def inner_of(trial, orbitals):
    high = orbitals.astype(BF16)
    low = (orbitals - high.astype(F32)).astype(BF16)
    return mul(trial, high, TN) + mul(trial, low, TN)


def correction(inner):
    size = inner.shape[0]
    row = lax.broadcasted_iota(jnp.int32, (128, 128), 0)
    col = lax.broadcasted_iota(jnp.int32, (128, 128), 1)
    on = row == col
    diagonal = [
        jnp.sum(jnp.where(on, inner[c : c + 128, c : c + 128], 0.0), axis=0, keepdims=True)
        for c in range(0, size, 128)
    ]
    inv = 1.0 / jnp.concatenate(diagonal, axis=1)
    row = lax.broadcasted_iota(jnp.int32, (size, size), 0)
    col = lax.broadcasted_iota(jnp.int32, (size, size), 1)
    on = row == col
    e1 = jnp.where(on, 1.0, 0.0) - inner * inv
    b1 = e1.astype(BF16)
    e2 = mul(b1, b1)
    b2 = e2.astype(BF16)
    both = mul(jnp.concatenate([b1, b2], axis=0), b2)
    g = e1 + e2 + both[:size]
    e4 = both[size:]
    return inv, g + e4 + short(g, e4)


def theta_kernel(turn, trial_hbm, walkers_hbm, theta, trial, walkers, idle, sems):
    rows = walkers.shape[0] // LOADS
    parts = [pl.ds(c * rows, rows) for c in range(LOADS)]
    copies = []
    for c, part in enumerate(parts):
        copies.append(
            (
                pltpu.make_async_copy(trial_hbm.at[part], trial.at[part], sems.at[0, c]),
                pltpu.make_async_copy(walkers_hbm.at[part], walkers.at[part], sems.at[1, c]),
            )
        )
        for copy in copies[-1]:
            copy.start()
    inner = None
    for c, part in enumerate(parts):
        for copy in copies[c]:
            copy.wait()
        piece = inner_of(trial[part, :], walkers[part, :])
        inner = piece if inner is None else inner + piece
    inv, f = correction(inner)
    scaled = walkers[...] * inv
    theta[...] = (scaled + short(scaled, f)).astype(BF16)
    if TURN:
        idle[...] = jnp.zeros_like(idle)

        def wait(_, carry):
            idle[...] = idle[...] + 1.0
            return carry

        lax.fori_loop(0, turn[0] * TURN, wait, 0)


def theta_call(turn, trial, walkers):
    m, n = walkers.shape
    return pl.pallas_call(
        theta_kernel,
        out_shape=jax.ShapeDtypeStruct((m, n), BF16),
        in_specs=[pl.BlockSpec(memory_space=pltpu.SMEM), AWAY, AWAY],
        out_specs=HERE,
        scratch_shapes=[
            VM(trial.shape, BF16),
            VM(walkers.shape, F32),
            VM((8, 128), F32),
            pltpu.SemaphoreType.DMA((2, LOADS)),
        ],
        compiler_params=grant(24),
        name="theta",
    )(turn, *away(trial, walkers))


def ready_kernel(chol_hbm, trial, flat_hbm, met_hbm, chol, flat, met, loads, stores):
    vectors, depth, width = chol.shape
    n = trial.shape[1]
    some = vectors // PIECES
    copies = []
    for c in range(PIECES):
        part = pl.ds(c * some, some)
        copies.append(pltpu.make_async_copy(chol_hbm.at[part], chol.at[part], loads.at[c]))
        copies[-1].start()
    sent = []
    for c in range(PIECES):
        part = pl.ds(c * some, some)
        copies[c].wait()
        turned = jnp.swapaxes(chol[part], 0, 1)
        for r in range(depth):
            flat[part, r * width : (r + 1) * width] = turned[r]
        sent.append(pltpu.make_async_copy(flat.at[part], flat_hbm.at[part], stores.at[0, c]))
        sent[-1].start()
        product = mul(turned.reshape(depth * some, width), trial[...]).astype(BF16)
        for r in range(depth):
            met[part, r * n : (r + 1) * n] = product[r * some : (r + 1) * some]
        sent.append(pltpu.make_async_copy(met.at[part], met_hbm.at[part], stores.at[1, c]))
        sent[-1].start()
    for copy in sent:
        copy.wait()


def ready_call(chol, trial):
    vectors, depth, width = chol.shape
    n = trial.shape[1]
    return pl.pallas_call(
        ready_kernel,
        out_shape=(
            pltpu.HBM((vectors, depth * width), BF16),
            pltpu.HBM((vectors, depth * n), BF16),
        ),
        in_specs=[AWAY, HERE],
        out_specs=(AWAY, AWAY),
        scratch_shapes=[
            VM(chol.shape, BF16),
            VM((vectors, depth * width), BF16),
            VM((vectors, depth * n), BF16),
            pltpu.SemaphoreType.DMA((PIECES,)),
            pltpu.SemaphoreType.DMA((2, PIECES)),
        ],
        compiler_params=grant(24),
        name="ready",
    )(*away(chol), *near(trial))


def bias_kernel(theta, met_hbm, extra, out, rows, met, sems):
    walkers, depth, n = theta.shape
    some = met.shape[0] // PIECES
    copies = []
    for c in range(PIECES):
        part = pl.ds(c * some, some)
        copies.append(pltpu.make_async_copy(met_hbm.at[part], met.at[part], sems.at[c]))
        copies[-1].start()
    turned = jnp.swapaxes(theta[...], 0, 1)
    for r in range(depth):
        rows[:, r * n : (r + 1) * n] = turned[r]
    for copy in copies:
        copy.wait()
    total = mul(rows[...], met[...], NT).astype(out.dtype)
    for c in range(out.shape[0]):
        out[c, :walkers, :] = total
        out[c, walkers:, :] = extra[...]


def bias_call(theta, met, extra, copies):
    walkers, depth, n = theta.shape
    vectors = met.shape[0]
    return pl.pallas_call(
        bias_kernel,
        out_shape=jax.ShapeDtypeStruct((copies, walkers + extra.shape[0], vectors), extra.dtype),
        in_specs=[HERE, AWAY, HERE],
        out_specs=HERE,
        scratch_shapes=[
            VM((walkers, depth * n), BF16),
            VM(met.shape, BF16),
            pltpu.SemaphoreType.DMA((PIECES,)),
        ],
        compiler_params=grant(16),
        name="bias",
    )(*near(theta), *away(met), *near(extra))


def spread_kernel(parts, out):
    total = jnp.sum(parts[...].astype(F32), axis=0).astype(out.dtype)
    for c in range(out.shape[0]):
        out[c] = total


def spread_call(parts, copies):
    return pl.pallas_call(
        spread_kernel,
        out_shape=jax.ShapeDtypeStruct((copies,) + parts.shape[1:], parts.dtype),
        in_specs=[HERE],
        out_specs=HERE,
        compiler_params=grant(8),
        name="spread",
    )(*near(parts))


def operator_kernel(parts, fields, chol, operator, summed, rows, turned, sems):
    total = jnp.sum(parts[...].astype(F32), axis=0)
    summed[...] = total
    walkers, depth, width = operator.shape
    shifted = (fields[...] + root_step * total[:walkers]).astype(BF16)
    some = width // PIECES
    copies = []
    for c in range(PIECES):
        part = pl.ds(c * some, some)
        for r in range(depth):
            start = r * width + c * some
            rows[r, :, part] = (root_step * mul(shifted, chol[:, start : start + some])).astype(BF16)
        turned[:, :, part] = jnp.swapaxes(rows[:, :, part], 0, 1)
        copies.append(pltpu.make_async_copy(turned.at[:, :, part], operator.at[:, :, part], sems.at[c]))
        copies[-1].start()
    for copy in copies:
        copy.wait()


def operator_call(parts, fields, chol, depth):
    walkers = fields.shape[0]
    width = chol.shape[1] // depth
    return pl.pallas_call(
        operator_kernel,
        out_shape=(
            pltpu.HBM((walkers, depth, width), BF16),
            jax.ShapeDtypeStruct(parts.shape[1:], F32),
        ),
        in_specs=[HERE] * 3,
        out_specs=(AWAY, HERE),
        scratch_shapes=[
            VM((depth, walkers, width), BF16),
            VM((walkers, depth, width), BF16),
            pltpu.SemaphoreType.DMA((PIECES,)),
        ],
        compiler_params=grant(20),
        name="operator",
    )(*near(parts, fields, chol))


def step_kernel(operator_hbm, trial, walkers, total, half, operator, term, now, done, sems):
    size, n = walkers.shape
    blocks, depth, _ = operator.shape
    rows = size // PIECES
    parts = [pl.ds(c * rows, rows) for c in range(PIECES)]
    some = blocks // LOADS
    tall = size // LOADS
    copies = []
    for c in range(LOADS):
        part = pl.ds(c * some, some)
        copies.append(
            pltpu.make_async_copy(operator_hbm.at[part], operator.at[part], sems.at[0, c])
        )
        copies[-1].start()
    start = walkers[...].astype(BF16)
    for c in range(LOADS):
        part = pl.ds(c * tall, tall)
        copies[c].wait()
        fresh = mul(operator[c * some : (c + 1) * some].reshape(tall, size), start)
        term[part, :] = fresh.astype(BF16)
        now[part, :] = walkers[part, :] + fresh
    full = now[...]
    last = term[...]
    for order in range(2, TAYLOR + 1):
        fresh = mul(operator[...].reshape(size, size), last) / float(order)
        full = full + fresh
        last = fresh.astype(BF16)
    now[...] = full
    copies = [pltpu.make_async_copy(now, total, sems.at[1, PIECES])]
    copies[0].start()
    inv, f = correction(inner_of(trial[...], now[...]))
    for c, part in enumerate(parts):
        scaled = now[part, :] * inv
        done[part, :] = scaled + short(scaled, f)
        copies.append(pltpu.make_async_copy(done.at[part, :], half.at[part, :], sems.at[1, c]))
        copies[-1].start()
    for copy in copies:
        copy.wait()


def step_call(operator, trial, walkers):
    return pl.pallas_call(
        step_kernel,
        out_shape=(jax.ShapeDtypeStruct(walkers.shape, F32),) * 2,
        in_specs=[AWAY, HERE, HERE],
        out_specs=(AWAY, AWAY),
        scratch_shapes=[
            VM(operator.shape, BF16),
            VM(walkers.shape, BF16),
            VM(walkers.shape, F32),
            VM(walkers.shape, F32),
            pltpu.SemaphoreType.DMA((2, PIECES + 1)),
        ],
        compiler_params=grant(30),
        name="step",
    )(*away(operator), *near(trial, walkers))


def swap(array, axes):
    return lax.all_to_all(array, axes, split_axis=0, concat_axis=0, tiled=True)


def per_device(chol, trial, walkers, fields, weights):
    _, _, n = walkers.shape
    vectors, depth, _ = chol.shape
    group = lax.axis_size(PAIR)
    place = lax.axis_index(PAIR)
    orbitals = walkers[0]
    turn = lax.axis_index("grp_1").astype(jnp.int32).reshape(1)
    theta = theta_call(turn, trial, orbitals).reshape(group, depth, n)
    theta_block = swap(theta, PAIR)
    flat, met = ready_call(chol, trial)
    row = lax.broadcasted_iota(jnp.int32, (16, vectors), 0)
    lane = lax.broadcasted_iota(jnp.int32, (16, vectors), 1)
    weight = weights[0]
    high = lax.reduce_precision(weight, 8, 7)
    middle = lax.reduce_precision(weight - high, 8, 7)
    low = weight - high - middle
    pieces = jnp.where(row == 0, high, jnp.where(row == 1, middle, jnp.where(row == 2, low, 0.0)))
    extra = jnp.where(lane == place, pieces, 0.0).astype(BF16)
    parts = bias_call(theta_block, met, extra, lax.axis_size(FAR))
    parts = spread_call(swap(parts, FAR), lax.axis_size(NEAR))
    op_block, summed = operator_call(swap(parts, NEAR), fields, flat, depth)
    operator = swap(op_block, PAIR)
    total, half_green = step_call(operator, trial, orbitals)
    xbar = -root_step * summed[:group]
    growth = jnp.exp(jnp.sum(fields * xbar - 0.5 * xbar * xbar, axis=1))
    whole = jnp.sum(jnp.sum(summed[group:, :group], axis=0) * growth)
    for axis in GRP:
        whole = lax.psum(whole, axis)
    raw = weights * lax.dynamic_slice_in_dim(growth, place, 1, 0)
    new_weights = raw * (group * lax.axis_size(GRP) / whole)
    return (total[None], half_green[None], new_weights)


def solution(mesh):
    torus = Mesh(
        mesh.devices.reshape(2, 2, 4, 2, 8), ("grp_0", "grp_1", "pair_0", "pair_1", "pair_2")
    )
    every = GRP + PAIR
    return jax.shard_map(
        per_device,
        mesh=torus,
        in_specs=(P(None, PAIR, None), P(), P(every, None, None), P(GRP, None), P(every)),
        out_specs=(P(every, None, None), P(every, None, None), P(every)),
        check_vma=False,
    )
```
